32 devices in a mesh: section: 2 (over x), dp: 16 (over z, y, core).
Axes of the slice: x: 2, y: 2, z: 4, core: 2. Of those that a mesh axis runs over, the one named last changes fastest.
Arguments:
- saved_input: bfloat16 [2, 6144, 4096], P('section', 'dp'), may hold values from -8 to 8
- out_grad: bfloat16 [2, 6144, 768], P('section', 'dp'), may hold values from -8 to 8
- key_weight: bfloat16 [2, 4096, 768], P('section'), may hold values from -0.09375 to 0.09375
- layer_gate: float32 [2, 4096], P('section'), may hold values from 0.75 to 1
- q_prev: float32 [2, 768, 32], P('section'), may hold values from -0.21875 to 0.21875
- error_prev: bfloat16 [2, 16, 4096, 768], P('section', 'dp'), may hold values from -4 to 4
Outputs:
- upstream: bfloat16 [2, 6144, 4096], P('section', 'dp')
- p_basis: float32 [2, 4096, 32], P('section')
- q_factor: float32 [2, 768, 32], P('section')
- error_next: bfloat16 [2, 16, 4096, 768], P('section', 'dp')
The draws below stay inside these ranges and needn't reach their ends.
All inputs are finite; a program needn't handle non-finite values.
Results may differ from the reference program's by a relative error of at most 0.0034.
Values may be sent and summed in bfloat16 or wider, within the bound.
No kernel may reach another device: no remote copies, remote signals or barrier semaphores. Data moves between devices by JAX's collectives and lax.ppermute only.
A program may use at most 192 MiB of HBM per device.

```python
import math
import jax
import jax.numpy as jnp
from jax import lax

DW = 4096
KVW = 768
RANK = 32
TOK_DEV = 384
SECTIONS = 2
REPLICAS = 16
TOKENS = 6144


shared_count = 4


def rough_values(key, shape):
    return jax.random.normal(key, shape, jnp.float32)


def shared_parts(key):
    base = jax.random.fold_in(key, 4111)
    coeff_key, left_key, right_key = jax.random.split(base, 3)
    strength = math.sqrt(0.5 / math.sqrt(TOK_DEV))
    coeffs = rough_values(coeff_key, (SECTIONS, TOKENS, shared_count))
    left_dirs = jax.random.normal(left_key, (SECTIONS, DW, shared_count), jnp.float32) * strength
    right_dirs = jax.random.normal(right_key, (SECTIONS, KVW, shared_count), jnp.float32) * strength
    return (coeffs, left_dirs, right_dirs)


def draw_saved_input(key, part):
    coeffs, left_dirs, right_dirs = shared_parts(key)
    noise_part = rough_values(jax.random.fold_in(key, 17), (SECTIONS, TOKENS, DW))
    values = 0.9 * noise_part + jnp.einsum('stc,sdc->std', coeffs, left_dirs)
    return jnp.clip(values, -8.0, 8.0).astype(jnp.bfloat16)


def draw_out_grad(key, part):
    coeffs, left_dirs, right_dirs = shared_parts(key)
    noise_part = rough_values(jax.random.fold_in(key, 29), (SECTIONS, TOKENS, KVW))
    values = 0.9 * noise_part + jnp.einsum('stc,skc->stk', coeffs, right_dirs)
    return jnp.clip(values, -8.0, 8.0).astype(jnp.bfloat16)


def level_of(key, dims, cuts, smallest, largest):
    def one(dim, blocks):
        heights = jax.random.uniform(jax.random.fold_in(jax.random.fold_in(key, 6), dim), (blocks,), jnp.float32, smallest / len(cuts), largest / len(cuts))
        return jnp.repeat(jnp.exp(heights), dims[dim] // blocks).reshape((-1,) + (1,) * (len(dims) - dim - 1))

    loudness = one(*cuts[0])
    for cut in cuts[1:]:
        loudness = loudness * one(*cut)
    return loudness


def noise(stream_key, dims, width, bound, shards=(), held_as=jnp.bfloat16):
    array = width * jax.random.normal(stream_key, dims, jnp.float32)
    if shards:
        array = array * level_of(stream_key, dims, shards, -0.22, 0.18)
    return jnp.clip(array, -bound, bound).astype(held_as)


def setup_inputs(seed: int = 0) -> dict:
    streams_of = jax.random.split(jax.random.key(seed), 7)
    saved_input = draw_saved_input(jax.random.fold_in(streams_of[6], 71), 0)
    out_grad = draw_out_grad(jax.random.fold_in(streams_of[6], 71), 0)
    key_weight = noise(streams_of[2], (SECTIONS, DW, KVW), DW ** -0.5, 0.09375, ((0, 2),))
    layer_gate = jnp.clip(jnp.exp(math.log(1.0) - 0.2876821 * jax.random.uniform(streams_of[3], (SECTIONS, DW), jnp.float32) ** level_of(streams_of[3], (SECTIONS, DW), ((0, 2),), -0.2, 0.2)), 0.75, 1.0)
    q_prev = noise(streams_of[4], (SECTIONS, KVW, RANK), KVW ** -0.5, 0.21875, ((0, 2),), jnp.float32)
    error_prev = noise(streams_of[5], (SECTIONS, REPLICAS, DW, KVW), 0.5, 4.0, ((0, 2), (1, 16)))
    return {"saved_input": saved_input, "out_grad": out_grad, "key_weight": key_weight, "layer_gate": layer_gate, "q_prev": q_prev, "error_prev": error_prev}


highest = lax.Precision.HIGHEST

def orthonormal(p_mean):
    gram_matrix = jnp.dot(p_mean.T, p_mean, precision=highest)
    triangle = jnp.linalg.cholesky(gram_matrix)
    return lax.linalg.triangular_solve(triangle, p_mean, left_side=False, lower=True, transpose_a=True)

def reference(saved_input, out_grad, key_weight, layer_gate, q_prev, error_prev):
    norm_scale = 1.0 / math.sqrt(TOK_DEV)
    bases = []
    factors = []
    errors = []
    uppers = []
    carried = jnp.zeros((TOKENS, DW), jnp.bfloat16)
    for segment in reversed(range(SECTIONS)):
        inputs = saved_input[segment].reshape(REPLICAS, TOK_DEV, DW).astype(jnp.float32)
        grads = out_grad[segment].reshape(REPLICAS, TOK_DEV, KVW).astype(jnp.float32)
        merged = jnp.einsum('rtd,rtk->rdk', inputs, grads, precision=highest) * norm_scale
        merged = merged + error_prev[segment].astype(jnp.float32)
        p_mean = jnp.einsum('rdk,kc->dc', merged, q_prev[segment], precision=highest) / REPLICAS
        basis = orthonormal(p_mean)
        q_mean = jnp.einsum('rdk,dc->kc', merged, basis, precision=highest) / REPLICAS
        approx = jnp.dot(basis, q_mean.T, precision=highest)
        errors.append((merged - approx[None]).astype(jnp.bfloat16))
        bases.append(basis)
        factors.append(q_mean)
        branch = jnp.dot(out_grad[segment].astype(jnp.float32), key_weight[segment].T.astype(jnp.float32), preferred_element_type=jnp.float32)
        chain = layer_gate[segment][None, :] * (branch + carried.astype(jnp.float32))
        carried = chain.astype(jnp.bfloat16)
        uppers.append(carried)
    upstream = jnp.stack(uppers[::-1])
    p_basis = jnp.stack(bases[::-1])
    q_factor = jnp.stack(factors[::-1])
    error_next = jnp.stack(errors[::-1])
    return (upstream, p_basis, q_factor, error_next)
```

```python
import math

import jax
import jax.numpy as jnp
from jax import lax
from jax.sharding import PartitionSpec as P

highest = lax.Precision.HIGHEST


def thirds(x, axis):
    first = lax.reduce_precision(x, 8, 7)
    rest = x - first
    second = lax.reduce_precision(rest, 8, 7)
    third = rest - second
    return jnp.concatenate([first, second, third], axis).astype(jnp.bfloat16)


def fold_rows(x):
    n = x.shape[0] // 3
    return x[:n] + (x[n : 2 * n] + x[2 * n :])


def mm(a, b, ca, cb):
    return lax.dot_general(a, b, (((ca,), (cb,)), ((), ())), preferred_element_type=jnp.float32)


def flip(x, bit):
    n = lax.axis_size("dp")
    return lax.ppermute(x, "dp", [(i, i ^ (1 << bit)) for i in range(n)])


def my_bit(bit):
    return (lax.axis_index("dp") >> bit) & 1


def scatter_half(x, bit):
    n = x.shape[0] // 2
    mine = my_bit(bit)
    keep = lax.dynamic_slice_in_dim(x, mine * n, n, 0)
    send = lax.dynamic_slice_in_dim(x, (1 - mine) * n, n, 0)
    return keep + flip(send, bit)


def gather_half(x, bit):
    other = flip(x, bit)
    return jnp.where(
        my_bit(bit) == 0, jnp.concatenate([x, other], 0), jnp.concatenate([other, x], 0)
    )


def all_sum(x, scatter_bits):
    n = lax.axis_size("dp")
    bits = n.bit_length() - 1
    if n != 1 << bits:
        return lax.psum(x, "dp")
    split = [b for b in scatter_bits if b < bits]
    for b in split:
        x = scatter_half(x, b)
    for b in range(bits):
        if b not in split:
            x = x + flip(x, b)
    for b in reversed(split):
        x = gather_half(x, b)
    return x


def body(saved_input, out_grad, key_weight, layer_gate, q_prev, error_prev):
    inputs = saved_input[0]
    grads = out_grad[0]
    weights = key_weight[0]
    gate_row = layer_gate[0]
    right_prev = q_prev[0]
    error = error_prev[0, 0]
    replicas = lax.axis_size("dp")
    norm_scale = 1.0 / math.sqrt(inputs.shape[0])

    branch = mm(grads, weights, 1, 1)
    current = (gate_row[None, :] * branch).astype(jnp.bfloat16)
    sections = lax.axis_size("section")
    received = lax.ppermute(current, "section", [(i, i - 1) for i in range(1, sections)])

    q_t = thirds(right_prev.T, 0)
    gq = fold_rows(mm(q_t, grads, 1, 1)) * norm_scale
    left = fold_rows(mm(q_t, error, 1, 1) + mm(thirds(gq, 0), inputs, 1, 0))
    p_t = all_sum(left, (0, 1)) * (1.0 / replicas)

    merged = mm(inputs, grads, 0, 0) * norm_scale + error.astype(jnp.float32)

    p3 = thirds(p_t, 0)
    xp = fold_rows(mm(p3, inputs, 1, 1)) * norm_scale
    right = fold_rows(mm(p3, error, 1, 0) + mm(thirds(xp, 0), grads, 1, 0))
    r_t = all_sum(right, (0,)) * (1.0 / replicas)

    gram_matrix = lax.dot_general(p_t, p_t, (((1,), (1,)), ((), ())), precision=highest)
    triangle = jnp.linalg.cholesky(gram_matrix)
    inverse = lax.linalg.triangular_solve(
        triangle, jnp.eye(triangle.shape[0], dtype=jnp.float32), left_side=True, lower=True
    )
    basis_t = jnp.dot(inverse, p_t, precision=highest)
    right_t = jnp.dot(inverse, r_t, precision=highest)

    b3 = thirds(basis_t, 0)
    q3 = thirds(right_t, 0)
    k = basis_t.shape[0]
    left_terms = jnp.concatenate([b3, b3[: 2 * k], b3[:k]], 0)
    right_terms = jnp.concatenate(
        [q3[:k], q3[:k], q3[:k], q3[k : 2 * k], q3[k : 2 * k], q3[2 * k :]], 0
    )
    approx = mm(left_terms, right_terms, 0, 0)
    error_next = (merged - approx).astype(jnp.bfloat16)

    upper = (gate_row[None, :] * (branch + received.astype(jnp.float32))).astype(jnp.bfloat16)
    return (upper[None], basis_t.T[None], right_t.T[None], error_next[None, None])


def solution(mesh):
    return jax.shard_map(
        body,
        mesh=mesh,
        in_specs=(
            P("section", "dp", None),
            P("section", "dp", None),
            P("section", None, None),
            P("section", None),
            P("section", None, None),
            P("section", "dp", None, None),
        ),
        out_specs=(
            P("section", "dp", None),
            P("section", None, None),
            P("section", None, None),
            P("section", "dp", None, None),
        ),
        check_vma=False,
    )
```

```python
import functools
import math

import jax
import jax.numpy as jnp
from jax import lax
from jax.experimental import pallas as pl
from jax.experimental.pallas import tpu as pltpu
from jax.sharding import PartitionSpec as P

highest = lax.Precision.HIGHEST
f32 = jnp.float32
bf16 = jnp.bfloat16


def mm(a, b, ca, cb, precision=None):
    return lax.dot_general(
        a, b, (((ca,), (cb,)), ((), ())), preferred_element_type=f32, precision=precision
    )


def split(x, terms):
    out = []
    for _ in range(terms):
        out.append(x.astype(bf16))
        x = x - out[-1].astype(f32)
    return out


def thirds(x):
    return jnp.concatenate(split(x, 3), 0)


def fold(x):
    n = x.shape[0] // 3
    return x[:n] + (x[n : 2 * n] + x[2 * n :])


def place(me_ref, j, quarter):
    high = (me_ref[0] ^ (j >> 1)) * (2 * quarter)
    low = (me_ref[1] ^ (j & 1)) * quarter
    return pl.multiple_of(high + low, quarter)


def left_kernel(
    me_ref, q_ref, g_ref, x_hbm, e_hbm, keep_ref, send_ref, x_ref, e_ref, x_sem, e_sem, *, scale, steps,
):
    rank = q_ref.shape[0]
    quarter = rank // 4
    width = x_ref.shape[1] // steps
    copies = []
    for i in range(steps):
        at = pl.ds(i * width, width)
        copies.append(
            (
                pltpu.make_async_copy(e_hbm.at[at, :], e_ref.at[at, :], e_sem.at[i]),
                pltpu.make_async_copy(x_hbm.at[:, at], x_ref.at[:, at], x_sem.at[i]),
            )
        )
        for copy in copies[-1]:
            copy.start()
    rows = [q_ref[pl.ds(place(me_ref, j, quarter), quarter), :] for j in range(4)]
    q3 = thirds(jnp.concatenate(rows, 0))
    gq3 = thirds(fold(mm(q3, g_ref[...], 1, 1)) * scale)
    for i in range(steps):
        at = pl.ds(i * width, width)
        for copy in copies[i]:
            copy.wait()
        left = fold(mm(q3, e_ref[at, :], 1, 1) + mm(gq3, x_ref[:, at], 1, 0))
        keep_ref[:, at] = left[: rank // 2]
        send_ref[:, at] = left[rank // 2 :]


def in_order(me_ref, out_ref, pm_ref, py_ref, pc_ref, mean):
    quarter = pm_ref.shape[0]
    parts = [pm_ref[...], py_ref[...], pc_ref[:quarter, :], pc_ref[quarter:, :]]
    for j in range(4):
        out_ref[pl.ds(place(me_ref, j, quarter), quarter), :] = parts[j] * mean


def right_kernel(
    me_ref, pm_ref, py_ref, pc_ref, g_ref, x_ref, e_ref,
    keep_ref, send_ref, gram_ref, ord_ref, acc_ref, *, scale, mean,
):
    rank = ord_ref.shape[0]
    half = rank // 2
    in_order(me_ref, ord_ref, pm_ref, py_ref, pc_ref, mean)
    p3 = thirds(ord_ref[...])
    xp3 = thirds(fold(mm(p3, x_ref[...], 1, 1)) * scale)
    acc_ref[...] = fold(mm(p3, e_ref[...], 1, 0) + mm(xp3, g_ref[...], 1, 0)) * mean
    gram_ref[...] = mm(p3, p3, 1, 1)
    keep_ref[...] = acc_ref[pl.ds(pl.multiple_of(me_ref[0] * half, half), half), :]
    send_ref[...] = acc_ref[pl.ds(pl.multiple_of((1 - me_ref[0]) * half, half), half), :]


def factor_kernel(gram_ref, inv_ref):
    rank = inv_ref.shape[0]
    wide = fold(gram_ref[...])
    a = wide[:, :rank] + (wide[:, rank : 2 * rank] + wide[:, 2 * rank :])
    row = lax.broadcasted_iota(jnp.int32, (rank, rank), 0)
    col = lax.broadcasted_iota(jnp.int32, (rank, rank), 1)
    b = (row == col).astype(f32)
    pivots = jnp.ones((rank, rank), f32)
    for j in range(rank):
        pivot = a[j : j + 1, j : j + 1]
        pivots = jnp.where(row == j, pivot, pivots)
        ratio = jnp.where(row > j, a[:, j : j + 1] / pivot, 0.0)
        b = b - ratio * b[j : j + 1, :]
        a = a - ratio * a[j : j + 1, :]
    inv_ref[...] = b / jnp.sqrt(pivots)


def merged_kernel(x_ref, g_ref, e_ref, out_ref, *, scale, at):
    rows = out_ref.shape[0]
    x = x_ref[:, at : at + rows]
    out_ref[...] = mm(x, g_ref[...], 0, 0) * scale + e_ref[at : at + rows, :].astype(f32)


def basis_kernel(me_ref, inv_ref, pm_ref, py_ref, pc_ref, basis_ref, terms_ref, ord_ref, *, mean):
    in_order(me_ref, ord_ref, pm_ref, py_ref, pc_ref, mean)
    basis_t = mm(inv_ref[...], ord_ref[...], 1, 0, highest)
    basis_ref[...] = basis_t
    hi, lo = split(basis_t, 2)
    terms_ref[...] = jnp.concatenate([hi, lo, hi, jnp.zeros_like(hi)], 0).T


def final_kernel(me_ref, inv_ref, rk_ref, ro_ref, terms_ref, *rest, halves):
    merged_refs = rest[:halves]
    err_ref, q_ref, rt_ref, q3_ref = rest[halves:]
    half = rk_ref.shape[0]
    rows = err_ref.shape[0]

    @pl.when(pl.program_id(0) == 0)
    def _():
        rt_ref[pl.ds(pl.multiple_of(me_ref[0] * half, half), half), :] = rk_ref[...]
        rt_ref[pl.ds(pl.multiple_of((1 - me_ref[0]) * half, half), half), :] = ro_ref[...]
        q_t = mm(inv_ref[...], rt_ref[...], 1, 0, highest)
        q_ref[...] = q_t
        hi, lo = split(q_t, 2)
        q3_ref[...] = jnp.concatenate([hi, hi, lo, jnp.zeros_like(hi)], 0)

    per = merged_refs[0].shape[0] // rows
    i = pl.program_id(0)
    approx = mm(terms_ref[pl.ds(pl.multiple_of(i * rows, rows), rows), :], q3_ref[...], 1, 0)
    for h in range(halves):

        @pl.when(i // per == h)
        def _(h=h):
            at = pl.multiple_of((i - h * per) * rows, rows)
            err_ref[...] = (merged_refs[h][pl.ds(at, rows), :] - approx).astype(bf16)


def branch_kernel(gate_ref, g_ref, w_ref, out_ref):
    out_ref[...] = (gate_ref[...] * mm(g_ref[...], w_ref[...], 1, 1)).astype(bf16)


def upper_kernel(gate_ref, g_ref, w_ref, c_ref, *rest):
    out_ref = rest[-1]
    branch = mm(g_ref[...], w_ref[...], 1, 1)
    out_ref[...] = (gate_ref[...] * (branch + c_ref[...].astype(f32))).astype(bf16)


def whole(shape):
    return pl.BlockSpec(shape, lambda i: (0,) * len(shape))


def down(height, cols):
    return pl.BlockSpec((height, cols), lambda i: (i, 0))


smem = pl.BlockSpec(memory_space=pltpu.SMEM)
near = pl.BlockSpec(memory_space=pltpu.VMEM)
far_off = pl.BlockSpec(memory_space=pltpu.HBM)
plain = pltpu.CompilerParams(vmem_limit_bytes=24 << 20)
order = pltpu.CompilerParams(dimension_semantics=("arbitrary",), vmem_limit_bytes=24 << 20)


def flip(x, bit):
    n = lax.axis_size("dp")
    return lax.ppermute(x, "dp", [(i, i ^ (1 << bit)) for i in range(n)])


def step(saved_input, out_grad, key_weight, layer_gate, q_prev, error_prev):
    inputs = saved_input[0]
    grads = out_grad[0]
    weights = key_weight[0]
    gate_row = layer_gate
    right_prev = q_prev[0]
    error = error_prev[0, 0]
    tokens, wide = inputs.shape
    keys, rank = right_prev.shape
    right_t = right_prev.T
    half, quarter = rank // 2, rank // 4
    replicas = lax.axis_size("dp")
    bits = replicas.bit_length() - 1
    assert replicas == 1 << bits and bits >= 2
    scale = 1.0 / math.sqrt(tokens)
    mean = 1.0 / replicas
    weights = pltpu.with_memory_space_constraint(weights, pltpu.HBM)
    sections = lax.axis_size("section")
    route = [(i, i - 1) for i in range(1, sections)]
    place_in = lax.axis_index("dp")
    me = jnp.stack([place_in & 1, (place_in >> 1) & 1]).astype(jnp.int32)

    unit = wide // 4 if wide % 512 == 0 else wide
    cuts = [(0, 1), (2, 2), (1, 1)] if unit < wide else [(0, 1)]
    received = []
    for at, size in cuts:
        span = size * unit
        current = pl.pallas_call(
            branch_kernel,
            grid=(1,),
            in_specs=[
                pl.BlockSpec((1, span), lambda _, k=at // size: (0, k)),
                whole((tokens, keys)),
                pl.BlockSpec((span, keys), lambda _, k=at // size: (k, 0)),
            ],
            out_specs=whole((tokens, span)),
            out_shape=jax.ShapeDtypeStruct((tokens, span), bf16),
            compiler_params=order,
            name="branch",
        )(gate_row, grads, weights)
        received.append(lax.ppermute(current, "section", route))

    unit_steps = wide // unit
    keep, send, inputs_near, error_near = pl.pallas_call(
        functools.partial(left_kernel, scale=scale, steps=unit_steps),
        in_specs=[smem, near, near, far_off, far_off],
        out_specs=[near] * 4,
        out_shape=[
            pltpu.VMEM((half, wide), f32),
            pltpu.VMEM((half, wide), f32),
            pltpu.VMEM(inputs.shape, bf16),
            pltpu.VMEM(error.shape, bf16),
        ],
        scratch_shapes=[pltpu.SemaphoreType.DMA((unit_steps,)), pltpu.SemaphoreType.DMA((unit_steps,))],
        compiler_params=plain,
        name="left",
    )(me, right_t, grads, inputs, error)

    chip = keep + flip(send, 0)
    mine = chip[:quarter] + flip(chip[quarter:], 1)
    for b in range(2, bits):
        mine = mine + flip(mine, b)
    beside = flip(mine, 1)
    far = flip(jnp.concatenate([mine, beside], 0), 0)

    merged = []
    for h in range(2):
        rows = wide // 2
        merged.append(
            pl.pallas_call(
                functools.partial(merged_kernel, scale=scale, at=h * rows),
                in_specs=[near] * 3,
                out_specs=near,
                out_shape=pltpu.VMEM((rows, keys), f32),
                compiler_params=plain,
                name="merged",
            )(inputs_near, grads, error_near)
        )

    keep, send, gram = pl.pallas_call(
        functools.partial(right_kernel, scale=scale, mean=mean),
        in_specs=[smem] + [near] * 6,
        out_specs=[near] * 3,
        out_shape=[pltpu.VMEM((half, keys), f32)] * 2 + [pltpu.VMEM((3 * rank, 3 * rank), f32)],
        scratch_shapes=[pltpu.VMEM((rank, wide), f32), pltpu.VMEM((rank, keys), f32)],
        compiler_params=plain,
        name="right",
    )(me, mine, beside, far, grads, inputs_near, error_near)

    total = keep + flip(send, 0)
    for b in range(1, bits):
        total = total + flip(total, b)
    other = flip(total, 0)

    inverse = pl.pallas_call(
        factor_kernel,
        out_shape=jax.ShapeDtypeStruct((rank, rank), f32),
        compiler_params=pltpu.CompilerParams(vmem_limit_bytes=4 << 20),
        name="factor",
    )(gram)

    basis_t, terms = pl.pallas_call(
        functools.partial(basis_kernel, mean=mean),
        in_specs=[smem] + [near] * 4,
        out_specs=[near] * 2,
        out_shape=[jax.ShapeDtypeStruct((rank, wide), f32), pltpu.VMEM((wide, 4 * rank), bf16)],
        scratch_shapes=[pltpu.VMEM((rank, wide), f32)],
        compiler_params=plain,
        name="basis",
    )(me, inverse, mine, beside, far)

    error_next, q_t = pl.pallas_call(
        functools.partial(final_kernel, halves=2),
        grid=(unit_steps,),
        in_specs=[smem] + [near] * 6,
        out_specs=[down(unit, keys), whole((rank, keys))],
        out_shape=[
            jax.ShapeDtypeStruct((wide, keys), bf16),
            jax.ShapeDtypeStruct((rank, keys), f32),
        ],
        scratch_shapes=[pltpu.VMEM((rank, keys), f32), pltpu.VMEM((4 * rank, keys), bf16)],
        compiler_params=order,
        name="final",
    )(me, inverse, total, other, terms, *merged)

    upper = None
    for n, (at, size) in enumerate(cuts):
        span = size * unit
        block = pl.BlockSpec((tokens, span), lambda _, k=at // size: (0, k))
        specs = [
            pl.BlockSpec((1, span), lambda _, k=at // size: (0, k)),
            whole((tokens, keys)),
            pl.BlockSpec((span, keys), lambda _, k=at // size: (k, 0)),
            whole((tokens, span)),
        ]
        held = () if upper is None else (upper,)
        upper = pl.pallas_call(
            upper_kernel,
            grid=(1,),
            in_specs=specs + [pl.BlockSpec(memory_space=pl.ANY)] * len(held),
            out_specs=block,
            out_shape=jax.ShapeDtypeStruct((tokens, wide), bf16),
            input_output_aliases={4: 0} if held else {},
            compiler_params=order,
            name="upper",
        )(gate_row, grads, weights, received[n], *held)
    return (upper[None], basis_t.T[None], q_t.T[None], error_next[None, None])


def solution(mesh):
    return spread(mesh)


def spread(mesh):
    return jax.shard_map(
        step,
        mesh=mesh,
        in_specs=(
            P("section", "dp", None),
            P("section", "dp", None),
            P("section", None, None),
            P("section", None),
            P("section", None, None),
            P("section", "dp", None, None),
        ),
        out_specs=(
            P("section", "dp", None),
            P("section", None, None),
            P("section", None, None),
            P("section", "dp", None, None),
        ),
        check_vma=False,
    )
```

```python
import functools
import math

import jax
import jax.numpy as jnp
from jax import lax
from jax.experimental import pallas as pl
from jax.experimental.pallas import tpu as pltpu
from jax.sharding import PartitionSpec as P

highest = lax.Precision.HIGHEST
f32 = jnp.float32
bf16 = jnp.bfloat16


def mm(a, b, ca, cb, precision=None):
    return lax.dot_general(
        a, b, (((ca,), (cb,)), ((), ())), preferred_element_type=f32, precision=precision
    )


def split(x, terms):
    out = []
    for _ in range(terms):
        out.append(x.astype(bf16))
        x = x - out[-1].astype(f32)
    return out


def thirds(x):
    return jnp.concatenate(split(x, 3), 0)


def fold(x):
    n = x.shape[0] // 3
    return x[:n] + (x[n : 2 * n] + x[2 * n :])


def place(me_ref, j, quarter):
    high = (me_ref[0] ^ (j >> 1)) * (2 * quarter)
    low = (me_ref[1] ^ (j & 1)) * quarter
    return pl.multiple_of(high + low, quarter)


def left_kernel(
    me_ref, q_ref, g_ref, x_hbm, e_hbm, keep_ref, send_ref, x_ref, e_ref, x_sem, e_sem, *, scale, steps,
):
    rank = q_ref.shape[0]
    quarter = rank // 4
    width = x_ref.shape[1] // steps
    copies = []
    for i in range(steps):
        at = pl.ds(i * width, width)
        copies.append(
            (
                pltpu.make_async_copy(e_hbm.at[at, :], e_ref.at[at, :], e_sem.at[i]),
                pltpu.make_async_copy(x_hbm.at[:, at], x_ref.at[:, at], x_sem.at[i]),
            )
        )
        for copy in copies[-1]:
            copy.start()
    rows = [q_ref[pl.ds(place(me_ref, j, quarter), quarter), :] for j in range(4)]
    q3 = thirds(jnp.concatenate(rows, 0))
    gq3 = thirds(fold(mm(q3, g_ref[...], 1, 1)) * scale)
    for i in range(steps):
        at = pl.ds(i * width, width)
        for copy in copies[i]:
            copy.wait()
        left = fold(mm(q3, e_ref[at, :], 1, 1) + mm(gq3, x_ref[:, at], 1, 0))
        keep_ref[:, at] = left[: rank // 2]
        send_ref[:, at] = left[rank // 2 :]


def in_order(me_ref, out_ref, pm_ref, py_ref, pc_ref, mean):
    quarter = pm_ref.shape[0]
    parts = [pm_ref[...], py_ref[...], pc_ref[:quarter, :], pc_ref[quarter:, :]]
    for j in range(4):
        out_ref[pl.ds(place(me_ref, j, quarter), quarter), :] = parts[j] * mean


def right_kernel(
    me_ref, pm_ref, py_ref, pc_ref, g_ref, x_ref, e_ref,
    keep_ref, send_ref, gram_ref, ord_ref, acc_ref, *, scale, mean,
):
    rank = ord_ref.shape[0]
    half = rank // 2
    in_order(me_ref, ord_ref, pm_ref, py_ref, pc_ref, mean)
    p3 = thirds(ord_ref[...])
    xp3 = thirds(fold(mm(p3, x_ref[...], 1, 1)) * scale)
    acc_ref[...] = fold(mm(p3, e_ref[...], 1, 0) + mm(xp3, g_ref[...], 1, 0)) * mean
    gram_ref[...] = mm(p3, p3, 1, 1)
    keep_ref[...] = acc_ref[pl.ds(pl.multiple_of(me_ref[0] * half, half), half), :]
    send_ref[...] = acc_ref[pl.ds(pl.multiple_of((1 - me_ref[0]) * half, half), half), :]


def factor_kernel(gram_ref, inv_ref):
    rank = inv_ref.shape[0]
    wide = fold(gram_ref[...])
    a = wide[:, :rank] + (wide[:, rank : 2 * rank] + wide[:, 2 * rank :])
    row = lax.broadcasted_iota(jnp.int32, (rank, rank), 0)
    col = lax.broadcasted_iota(jnp.int32, (rank, rank), 1)
    b = (row == col).astype(f32)
    pivots = jnp.ones((rank, rank), f32)
    for j in range(rank):
        pivot = a[j : j + 1, j : j + 1]
        pivots = jnp.where(row == j, pivot, pivots)
        ratio = jnp.where(row > j, a[:, j : j + 1] / pivot, 0.0)
        b = b - ratio * b[j : j + 1, :]
        a = a - ratio * a[j : j + 1, :]
    inv_ref[...] = b / jnp.sqrt(pivots)


def merged_kernel(x_ref, g_ref, e_ref, out_ref, *, scale, at):
    rows = out_ref.shape[0]
    x = x_ref[:, at : at + rows]
    out_ref[...] = mm(x, g_ref[...], 0, 0) * scale + e_ref[at : at + rows, :].astype(f32)


def basis_kernel(me_ref, inv_ref, pm_ref, py_ref, pc_ref, basis_ref, terms_ref, ord_ref, *, mean):
    in_order(me_ref, ord_ref, pm_ref, py_ref, pc_ref, mean)
    basis_t = mm(inv_ref[...], ord_ref[...], 1, 0, highest)
    basis_ref[...] = basis_t
    hi, lo = split(basis_t, 2)
    terms_ref[...] = jnp.concatenate([hi, lo, hi, jnp.zeros_like(hi)], 0).T


def final_kernel(me_ref, inv_ref, rk_ref, ro_ref, terms_ref, *rest, halves):
    merged_refs = rest[:halves]
    err_ref, q_ref, rt_ref, q3_ref = rest[halves:]
    half = rk_ref.shape[0]
    rows = err_ref.shape[0]

    @pl.when(pl.program_id(0) == 0)
    def _():
        rt_ref[pl.ds(pl.multiple_of(me_ref[0] * half, half), half), :] = rk_ref[...]
        rt_ref[pl.ds(pl.multiple_of((1 - me_ref[0]) * half, half), half), :] = ro_ref[...]
        q_t = mm(inv_ref[...], rt_ref[...], 1, 0, highest)
        q_ref[...] = q_t
        hi, lo = split(q_t, 2)
        q3_ref[...] = jnp.concatenate([hi, hi, lo, jnp.zeros_like(hi)], 0)

    per = merged_refs[0].shape[0] // rows
    i = pl.program_id(0)
    approx = mm(terms_ref[pl.ds(pl.multiple_of(i * rows, rows), rows), :], q3_ref[...], 1, 0)
    for h in range(halves):

        @pl.when(i // per == h)
        def _(h=h):
            at = pl.multiple_of((i - h * per) * rows, rows)
            err_ref[...] = (merged_refs[h][pl.ds(at, rows), :] - approx).astype(bf16)


def branch_kernel(gate_ref, g_ref, w_ref, c_ref, branch_ref):
    branch = mm(g_ref[...], w_ref[...], 1, 1)
    branch_ref[...] = branch
    c_ref[...] = (gate_ref[...] * branch).astype(bf16)


def upper_kernel(gate_ref, branch_ref, c_ref, *rest):
    rest[-1][...] = (gate_ref[...] * (branch_ref[...] + c_ref[...].astype(f32))).astype(bf16)


def whole(shape):
    return pl.BlockSpec(shape, lambda i: (0,) * len(shape))


def down(height, cols):
    return pl.BlockSpec((height, cols), lambda i: (i, 0))


smem = pl.BlockSpec(memory_space=pltpu.SMEM)
near = pl.BlockSpec(memory_space=pltpu.VMEM)
far_off = pl.BlockSpec(memory_space=pltpu.HBM)
plain = pltpu.CompilerParams(vmem_limit_bytes=24 << 20)
order = pltpu.CompilerParams(dimension_semantics=("arbitrary",), vmem_limit_bytes=24 << 20)


def flip(x, bit):
    n = lax.axis_size("dp")
    return lax.ppermute(x, "dp", [(i, i ^ (1 << bit)) for i in range(n)])


def step(saved_input, out_grad, key_weight, layer_gate, q_prev, error_prev):
    inputs = saved_input[0]
    grads = out_grad[0]
    weights = key_weight[0]
    gate_row = layer_gate
    right_prev = q_prev[0]
    error = error_prev[0, 0]
    tokens, wide = inputs.shape
    keys, rank = right_prev.shape
    right_t = right_prev.T
    half, quarter = rank // 2, rank // 4
    replicas = lax.axis_size("dp")
    bits = replicas.bit_length() - 1
    assert replicas == 1 << bits and bits >= 2
    scale = 1.0 / math.sqrt(tokens)
    mean = 1.0 / replicas
    weights, inputs, error, grads_far, gate_far = [
        pltpu.with_memory_space_constraint(a, pltpu.HBM)
        for a in (weights, inputs, error, grads, gate_row)
    ]
    sections = lax.axis_size("section")
    route = [(i, i - 1) for i in range(1, sections)]
    place_in = lax.axis_index("dp")
    me = jnp.stack([place_in & 1, (place_in >> 1) & 1]).astype(jnp.int32)

    unit = wide // 4 if wide % 512 == 0 else wide
    part = wide // 8 if wide % 1024 == 0 else wide
    cuts = [(0, 1), (1, 1), (4, 4), (2, 2)] if part < wide else [(0, 1)]
    branches = []
    received = []
    for at, size in cuts:
        span = size * part
        current, branch = pl.pallas_call(
            branch_kernel,
            grid=(1,),
            in_specs=[
                pl.BlockSpec((1, span), lambda _, k=at // size: (0, k)),
                whole((tokens, keys)),
                pl.BlockSpec((span, keys), lambda _, k=at // size: (k, 0)),
            ],
            out_specs=[whole((tokens, span)), near],
            out_shape=[jax.ShapeDtypeStruct((tokens, span), bf16), pltpu.VMEM((tokens, span), f32)],
            compiler_params=order,
            name="branch",
        )(gate_far, grads_far, weights)
        branches.append(branch)
        received.append(lax.ppermute(current, "section", route))

    unit_steps = wide // unit
    left_steps = wide // part
    keep, send, inputs_near, error_near = pl.pallas_call(
        functools.partial(left_kernel, scale=scale, steps=left_steps),
        in_specs=[smem, near, near, far_off, far_off],
        out_specs=[near] * 4,
        out_shape=[
            pltpu.VMEM((half, wide), f32),
            pltpu.VMEM((half, wide), f32),
            pltpu.VMEM(inputs.shape, bf16),
            pltpu.VMEM(error.shape, bf16),
        ],
        scratch_shapes=[pltpu.SemaphoreType.DMA((left_steps,)), pltpu.SemaphoreType.DMA((left_steps,))],
        compiler_params=plain,
        name="left",
    )(me, right_t, grads, inputs, error)

    chip = keep + flip(send, 0)
    mine = chip[:quarter] + flip(chip[quarter:], 1)
    for b in range(2, bits):
        mine = mine + flip(mine, b)
    beside = flip(mine, 1)
    far = flip(jnp.concatenate([mine, beside], 0), 0)

    merged = []
    for h in range(2):
        rows = wide // 2
        merged.append(
            pl.pallas_call(
                functools.partial(merged_kernel, scale=scale, at=h * rows),
                in_specs=[near] * 3,
                out_specs=near,
                out_shape=pltpu.VMEM((rows, keys), f32),
                compiler_params=plain,
                name="merged",
            )(inputs_near, grads, error_near)
        )

    keep, send, gram = pl.pallas_call(
        functools.partial(right_kernel, scale=scale, mean=mean),
        in_specs=[smem] + [near] * 6,
        out_specs=[near] * 3,
        out_shape=[pltpu.VMEM((half, keys), f32)] * 2 + [pltpu.VMEM((3 * rank, 3 * rank), f32)],
        scratch_shapes=[pltpu.VMEM((rank, wide), f32), pltpu.VMEM((rank, keys), f32)],
        compiler_params=plain,
        name="right",
    )(me, mine, beside, far, grads, inputs_near, error_near)

    total = keep + flip(send, 0)
    for b in range(1, bits):
        total = total + flip(total, b)
    other = flip(total, 0)

    inverse = pl.pallas_call(
        factor_kernel,
        out_shape=jax.ShapeDtypeStruct((rank, rank), f32),
        compiler_params=pltpu.CompilerParams(vmem_limit_bytes=4 << 20),
        name="factor",
    )(gram)

    basis_t, terms = pl.pallas_call(
        functools.partial(basis_kernel, mean=mean),
        in_specs=[smem] + [near] * 4,
        out_specs=[near] * 2,
        out_shape=[jax.ShapeDtypeStruct((rank, wide), f32), pltpu.VMEM((wide, 4 * rank), bf16)],
        scratch_shapes=[pltpu.VMEM((rank, wide), f32)],
        compiler_params=plain,
        name="basis",
    )(me, inverse, mine, beside, far)

    error_next, q_t = pl.pallas_call(
        functools.partial(final_kernel, halves=2),
        grid=(unit_steps,),
        in_specs=[smem] + [near] * 6,
        out_specs=[down(unit, keys), whole((rank, keys))],
        out_shape=[
            jax.ShapeDtypeStruct((wide, keys), bf16),
            jax.ShapeDtypeStruct((rank, keys), f32),
        ],
        scratch_shapes=[pltpu.VMEM((rank, keys), f32), pltpu.VMEM((4 * rank, keys), bf16)],
        compiler_params=order,
        name="final",
    )(me, inverse, total, other, terms, *merged)

    upper = None
    for n, (at, size) in enumerate(cuts):
        span = size * part
        block = pl.BlockSpec((tokens, span), lambda _, k=at // size: (0, k))
        specs = [
            pl.BlockSpec((1, span), lambda _, k=at // size: (0, k)),
            near,
            whole((tokens, span)),
        ]
        held = () if upper is None else (upper,)
        upper = pl.pallas_call(
            upper_kernel,
            grid=(1,),
            in_specs=specs + [pl.BlockSpec(memory_space=pl.ANY)] * len(held),
            out_specs=block,
            out_shape=jax.ShapeDtypeStruct((tokens, wide), bf16),
            input_output_aliases={3: 0} if held else {},
            compiler_params=order,
            name="upper",
        )(gate_far, branches[n], received[n], *held)
    return (upper[None], basis_t.T[None], q_t.T[None], error_next[None, None])


def solution(mesh):
    return spread(mesh)


def spread(mesh):
    return jax.shard_map(
        step,
        mesh=mesh,
        in_specs=(
            P("section", "dp", None),
            P("section", "dp", None),
            P("section", None, None),
            P("section", None),
            P("section", None, None),
            P("section", "dp", None, None),
        ),
        out_specs=(
            P("section", "dp", None),
            P("section", None, None),
            P("section", None, None),
            P("section", "dp", None, None),
        ),
        check_vma=False,
    )
```
